32 devices in a mesh: ctx: 8 (over z, x), grp: 4 (over y, core).
Axes of the slice: x: 2, y: 2, z: 4, core: 2. Of those that a mesh axis runs over, the one named last changes fastest.
Arguments:
- queries: bfloat16 [1024, 12288], P('ctx', 'grp'), parts along dimension 1, may hold values from -250 to 250
- keys: bfloat16 [2, 1024, 768], P(None, 'ctx', 'grp'), parts along dimension 2, may hold values from -6 to 6
- values: bfloat16 [2, 1024, 512], P(None, 'ctx', 'grp'), parts along dimension 2, may hold values from -6 to 6
- gate_logits: bfloat16 [1024, 192], P('ctx', 'grp'), parts along dimension 1, may hold values from -6 to 6
- sel_ids: int32 [64, 64], P('ctx', 'grp'), parts along dimension 1, may hold values from -1 to 31, as said below
- pos_k: bfloat16 [32, 768], P(None, 'grp'), parts along dimension 1, may hold values from -1 to 1
- pos_v: bfloat16 [32, 512], P(None, 'grp'), parts along dimension 1, may hold values from -1 to 1
- mix_k: bfloat16 [192, 768], P(None, 'grp'), parts along dimension 1, may hold values from -0.4375 to 0.4375
- mix_v: bfloat16 [128, 512], P(None, 'grp'), parts along dimension 1, may hold values from -0.5 to 0.5
Outputs:
- attended: bfloat16 [1024, 8192], P('ctx', 'grp'), parts along dimension 1
The draws below stay inside these ranges and needn't reach their ends.
There are 4 independent parts, one for each index of `grp`. The reference program is written for one: setup_inputs(seed, part) draws one part's arguments, and reference() takes and returns one part's arrays. A program takes and returns all parts, laid end to end along the dimension named above; each array names one. Nothing has to cross between parts.
Inputs may be any that keep to these rules, and one draw needn't show every extreme that they name: `sel_ids`: the first entry of a row is the block that holds the row's tokens. The other entries name distinct blocks that lie wholly before position 1024, or are -1 at the row's end; each row has at least 12 entries that are not -1. Over the 8 rows of one device, the entries after the first name at most 16 = min(64, 1 * 2 * 8) distinct blocks, at most 2 of them held by one device, and no block in more than 8 rows.
All inputs are finite; a program needn't handle non-finite values.
Results may differ from the reference program's by a relative error of at most 0.011.
Values may be sent and summed in bfloat16 or wider, within the bound.
No kernel may reach another device: no remote copies, remote signals or barrier semaphores. Data moves between devices by JAX's collectives and lax.ppermute only.
A program may use at most 128 MiB of HBM per device.

```python
import jax
import jax.numpy as jnp
from jax import lax

HEADS = 16
DK = 192
DV = 128
CMP_BLOCK = 32
SEL_BLOCK = 64
TOPN = 16
QRY_DEV = 128
QBLOCK = 16
CACHE_ROUNDS = 1
SPAN = 1024
ROUNDS = 2
CONTEXT = 2048
WINDOW = 512
BPP = 2
NBLK = 32
QB_DEV = 8
UNIQ = 16
N_CTX = 8


def draw_queries(key, part):
    normal_key = jax.random.fold_in(jax.random.fold_in(key, 11), 0)
    entries = jax.random.normal(normal_key, (SPAN, HEADS * DK), jnp.float32)
    entries = jnp.clip(entries, -6.0, 6.0)
    return entries.astype(jnp.bfloat16)


def draw_sel_ids(key, part):
    device_keys = jax.random.split(jax.random.fold_in(key, 23), N_CTX)

    def one_device(device_key, device_no):
        perm_key, base_key, count_key = jax.random.split(device_key, 3)
        holders = jax.random.permutation(perm_key, N_CTX)
        starts = jax.random.randint(base_key, (N_CTX,), 0, CACHE_ROUNDS * BPP)
        counts = jax.random.randint(count_key, (QB_DEV,), TOPN - TOPN // 4, TOPN + 1)
        counts = counts.at[0].set(TOPN)
        row_no = jnp.arange(QB_DEV)[:, None]
        column = jnp.arange(1, TOPN)[None, :]
        label_no = (row_no * (TOPN - 1) + column - 1) % UNIQ
        holder = holders[label_no % N_CTX]
        local_no = (starts[holder] + label_no // N_CTX) % (CACHE_ROUNDS * BPP)
        block_no = (local_no // BPP * N_CTX + holder) * BPP + local_no % BPP
        block_no = jnp.where(column < counts[:, None], block_no, -1)
        own_block = (CACHE_ROUNDS * SPAN + device_no * QRY_DEV + jnp.arange(QB_DEV) * QBLOCK) // SEL_BLOCK
        return jnp.concatenate([own_block[:, None], block_no], axis=1).astype(jnp.int32)
    table = jax.vmap(one_device)(device_keys, jnp.arange(N_CTX))
    return table.reshape(SPAN // QBLOCK, TOPN)


def block_levels(rng, shape, cuts, least, largest):
    loudness, own = 1.0, jax.random.fold_in(rng, 6)
    for axis_at, parts in cuts:
        draws = jnp.exp(jax.random.uniform(jax.random.fold_in(own, axis_at), (parts,), jnp.float32, least / len(cuts), largest / len(cuts)))
        loudness = loudness * jnp.repeat(draws, shape[axis_at] // parts).reshape([-1 if axis == axis_at else 1 for axis in range(len(shape))])
    return loudness


def centred(own_key, dims, scale, most, pieces=(), kind=jnp.bfloat16):
    array = jax.random.normal(own_key, dims, jnp.float32) * scale
    if len(pieces) > 0:
        array = block_levels(own_key, dims, pieces, -0.22, 0.18) * array
    return jnp.clip(array, min=-most, max=most).astype(kind)


def setup_inputs(seed: int = 0, part: int = 0) -> dict:
    key_list = jax.random.split(jax.random.key(seed), 10)
    part_keys = jax.random.split(jax.random.fold_in(key_list[9], part), 10)
    return {
        "queries": draw_queries(jax.random.fold_in(jax.random.fold_in(key_list[9], part), 71), part),
        "keys": centred(part_keys[1], (ROUNDS, SPAN, DK), 1.0, 6.0, ((1, 8),)),
        "values": centred(part_keys[2], (ROUNDS, SPAN, DV), 1.0, 6.0, ((1, 8),)),
        "gate_logits": centred(part_keys[3], (SPAN, 3 * HEADS), 1.5, 6.0, ((0, 8),)),
        "sel_ids": draw_sel_ids(jax.random.fold_in(jax.random.fold_in(key_list[9], part), 71), part),
        "pos_k": centred(part_keys[5], (CMP_BLOCK, DK), CMP_BLOCK ** -0.5, 1.0),
        "pos_v": centred(part_keys[6], (CMP_BLOCK, DV), CMP_BLOCK ** -0.5, 1.0),
        "mix_k": centred(part_keys[7], (DK, DK), DK ** -0.5, 0.4375),
        "mix_v": centred(part_keys[8], (DV, DV), DV ** -0.5, 0.5),
    }


def attention(query_rows, key_rows, value_rows, allowed, head_count):
    scores = jnp.dot(query_rows, key_rows.T, preferred_element_type=jnp.float32) * (query_rows.shape[1] ** -0.5)
    scores = scores.reshape(-1, head_count, key_rows.shape[0])
    scores = jnp.where(allowed[:, None, :], scores, -jnp.inf)
    highest = jnp.max(scores, axis=2, keepdims=True)
    weights = jnp.exp(scores - highest)
    totals = jnp.sum(weights, axis=2)
    rounded = weights.astype(jnp.bfloat16).reshape(-1, key_rows.shape[0])
    mixture = jnp.dot(rounded, value_rows, preferred_element_type=jnp.float32)
    return mixture.reshape(-1, head_count, value_rows.shape[1]) / totals[:, :, None]


def compress(rows, gains, mixing):
    count = rows.shape[0] // CMP_BLOCK
    blocks = rows.reshape(count, CMP_BLOCK, rows.shape[1]).astype(jnp.float32)
    pooled = jnp.einsum("bjd,jd->bd", blocks, gains.astype(jnp.float32)).astype(jnp.bfloat16)
    return jnp.dot(pooled, mixing, preferred_element_type=jnp.float32).astype(jnp.bfloat16)


def reference(queries, keys, values, gate_logits, sel_ids, pos_k, pos_v, mix_k, mix_v):
    key_flat = keys.reshape(CONTEXT, DK)
    value_flat = values.reshape(CONTEXT, DV)
    first_query = CACHE_ROUNDS * SPAN
    comp_keys = compress(key_flat, pos_k, mix_k)
    comp_values = compress(value_flat, pos_v, mix_v)
    comp_ends = jnp.arange(CONTEXT // CMP_BLOCK, dtype=jnp.int32) * CMP_BLOCK + (CMP_BLOCK - 1)
    rows_each = min(512, SPAN)

    def dense_branches(block_no):
        offset = (block_no * rows_each).astype(jnp.int32)
        query_rows = lax.dynamic_slice_in_dim(queries, offset, rows_each, 0).reshape(rows_each * HEADS, DK)
        query_pos = first_query + offset + jnp.arange(rows_each, dtype=jnp.int32)
        compressed = attention(query_rows, comp_keys, comp_values, comp_ends[None, :] <= query_pos[:, None], HEADS)
        window_start = (first_query + offset - WINDOW).astype(jnp.int32)
        near_keys = lax.dynamic_slice_in_dim(key_flat, window_start, rows_each + WINDOW, 0)
        near_values = lax.dynamic_slice_in_dim(value_flat, window_start, rows_each + WINDOW, 0)
        key_pos = window_start + jnp.arange(rows_each + WINDOW, dtype=jnp.int32)
        inside = (key_pos[None, :] <= query_pos[:, None]) & (key_pos[None, :] > query_pos[:, None] - WINDOW)
        sliding = attention(query_rows, near_keys, near_values, inside, HEADS)
        return compressed, sliding

    compressed, sliding = lax.map(dense_branches, jnp.arange(SPAN // rows_each, dtype=jnp.int32))
    compressed = compressed.reshape(SPAN, HEADS, DV)
    sliding = sliding.reshape(SPAN, HEADS, DV)
    key_blocks = key_flat.reshape(NBLK, SEL_BLOCK, DK)
    value_blocks = value_flat.reshape(NBLK, SEL_BLOCK, DV)

    def selected_branch(block_no):
        chosen = sel_ids[block_no]
        clipped = jnp.maximum(chosen, 0).astype(jnp.int32)
        near_keys = key_blocks[clipped].reshape(TOPN * SEL_BLOCK, DK)
        near_values = value_blocks[clipped].reshape(TOPN * SEL_BLOCK, DV)
        offset = (block_no * QBLOCK).astype(jnp.int32)
        query_rows = lax.dynamic_slice_in_dim(queries, offset, QBLOCK, 0).reshape(QBLOCK * HEADS, DK)
        query_pos = first_query + offset + jnp.arange(QBLOCK, dtype=jnp.int32)
        key_pos = (clipped[:, None] * SEL_BLOCK + jnp.arange(SEL_BLOCK, dtype=jnp.int32)[None, :]).reshape(-1)
        usable = jnp.repeat(chosen >= 0, SEL_BLOCK)
        allowed = usable[None, :] & (key_pos[None, :] <= query_pos[:, None])
        return attention(query_rows, near_keys, near_values, allowed, HEADS)

    selected = lax.map(selected_branch, jnp.arange(SPAN // QBLOCK, dtype=jnp.int32)).reshape(SPAN, HEADS, DV)
    gate_values = jax.nn.sigmoid(gate_logits.astype(jnp.float32)).reshape(SPAN, 3, HEADS)
    combined = (gate_values[:, 0, :, None] * compressed + gate_values[:, 1, :, None] * selected
                + gate_values[:, 2, :, None] * sliding)
    return combined.reshape(SPAN, HEADS * DV).astype(jnp.bfloat16)
```

```python
import jax
import jax.numpy as jnp
from jax import lax
from jax.experimental import pallas as pl
from jax.experimental.pallas import tpu as pltpu
from jax.sharding import PartitionSpec as P

HEADS = 16
DK = 192
DV = 128
CMP_BLOCK = 32
SEL_BLOCK = 64
QBLOCK = 16
SPREAD = 64


def shifted(value, axis, steps):
    count = lax.axis_size(axis)
    pairs = [(source, (source + steps) % count) for source in range(count)]
    return lax.ppermute(value, axis, pairs)


def attention(query_rows, key_rows, value_rows, allowed, head_count):
    scores = jnp.dot(query_rows, key_rows.T, preferred_element_type=jnp.float32) * query_rows.shape[
        1
    ] ** (-0.5)
    scores = scores.reshape(-1, head_count, key_rows.shape[0])
    scores = jnp.where(allowed[:, None, :], scores, -jnp.inf)
    highest = jnp.max(scores, axis=2, keepdims=True)
    weights = jnp.exp(scores - highest)
    totals = jnp.sum(weights, axis=2)
    rounded = weights.astype(jnp.bfloat16).reshape(-1, key_rows.shape[0])
    mixture = jnp.dot(rounded, value_rows, preferred_element_type=jnp.float32)
    return mixture.reshape(-1, head_count, value_rows.shape[1]) / totals[:, :, None]


def exchange_body(queries, keys, values, gate_logits, sel_ids, pos_k, pos_v, mix_k, mix_v):
    devices = lax.axis_size("ctx")
    myself = lax.axis_index("ctx")
    rounds = keys.shape[0]
    cached = rounds - 1
    tokens = keys.shape[1]
    scaling = DK ** (-0.5)
    query_rows = queries.reshape(tokens * HEADS, DK)
    query_pos = (cached * devices + myself) * tokens + jnp.arange(tokens, dtype=jnp.int32)
    paired = jnp.concatenate([keys, values], axis=2)
    earlier_rows = []
    for shift_by in range(1, 5):
        wrapped = myself + shift_by >= devices
        outgoing = jnp.where(wrapped, paired[0], paired[1])
        earlier_rows.append(shifted(outgoing, "ctx", shift_by))
    per_piece = tokens // CMP_BLOCK
    local_count = rounds * per_piece
    pooled_k = jnp.einsum(
        "bjd,jd->bd",
        keys.reshape(local_count, CMP_BLOCK, DK),
        pos_k,
        preferred_element_type=jnp.float32,
    ).astype(jnp.bfloat16)
    pooled_v = jnp.einsum(
        "bjd,jd->bd",
        values.reshape(local_count, CMP_BLOCK, DV),
        pos_v,
        preferred_element_type=jnp.float32,
    ).astype(jnp.bfloat16)
    comp_keys = jnp.dot(pooled_k, mix_k, preferred_element_type=jnp.float32).astype(jnp.bfloat16)
    comp_values = jnp.dot(pooled_v, mix_v, preferred_element_type=jnp.float32).astype(jnp.bfloat16)
    all_keys, all_values = (
        lax.all_gather(comp_keys, "ctx", axis=0, tiled=True),
        lax.all_gather(comp_values, "ctx", axis=0, tiled=True),
    )
    length = all_keys.shape[0]
    summed = jnp.zeros((tokens, HEADS, DV), jnp.float32)
    highest = jnp.full((tokens, HEADS), -jnp.inf, jnp.float32)
    totals = jnp.zeros((tokens, HEADS), jnp.float32)
    for low_row in range(0, length, 512):
        high_row = min(length, low_row + 512)
        key_index = low_row + jnp.arange(high_row - low_row, dtype=jnp.int32)
        holder = key_index // local_count
        within = key_index % local_count
        end_pos = (
            (within // per_piece * devices + holder) * tokens
            + (within % per_piece + 1) * CMP_BLOCK
            - 1
        )
        allowed = end_pos[None, :] <= query_pos[:, None]
        scores = (
            jnp.dot(query_rows, all_keys[low_row:high_row].T, preferred_element_type=jnp.float32)
            * scaling
        )
        scores = jnp.where(
            allowed[:, None, :], scores.reshape(tokens, HEADS, high_row - low_row), -jnp.inf
        )
        raised = jnp.maximum(highest, jnp.max(scores, axis=2))
        anchor = jnp.where(raised == -jnp.inf, 0.0, raised)
        weights = jnp.exp(scores - anchor[:, :, None])
        factor = jnp.exp(highest - anchor)
        totals = totals * factor + jnp.sum(weights, axis=2)
        mixture = jnp.dot(
            weights.astype(jnp.bfloat16).reshape(tokens * HEADS, high_row - low_row),
            all_values[low_row:high_row],
            preferred_element_type=jnp.float32,
        )
        summed = summed * factor[:, :, None] + mixture.reshape(tokens, HEADS, DV)
        highest = raised
    compressed = summed / totals[:, :, None]
    window_rows = jnp.concatenate(earlier_rows[::-1] + [paired[1]], axis=0)
    column = jnp.arange(5 * tokens, dtype=jnp.int32)[None, :]
    offsets = jnp.arange(tokens, dtype=jnp.int32)[:, None]
    inside = (column > offsets) & (column <= 4 * tokens + offsets)
    sliding = attention(query_rows, window_rows[:, :DK], window_rows[:, DK:], inside, HEADS)
    per_block = tokens // SEL_BLOCK
    groups = sel_ids.shape[0]
    listed = sel_ids.shape[1]
    remote = sel_ids[:, 1:].reshape(-1)
    entries = remote.shape[0]
    usable = remote >= 0
    clipped = jnp.maximum(remote, 0)
    holder_piece = clipped // per_block
    holder = holder_piece % devices
    local_block = holder_piece // devices * per_block + clipped % per_block
    distinct = min(SPREAD, cached * per_block * devices)
    per_owner = -(-distinct // devices)
    earlier = jnp.arange(entries)[None, :] < jnp.arange(entries)[:, None]
    same_owner = holder[:, None] == holder[None, :]
    key_blocks = keys.reshape(rounds * per_block, SEL_BLOCK, DK)
    value_blocks = values.reshape(rounds * per_block, SEL_BLOCK, DV)
    repeated = (remote[:, None] == remote[None, :]) & usable[None, :] & earlier
    leading = usable & ~jnp.any(repeated, axis=1)
    before = same_owner & leading[None, :] & earlier
    slot_of = holder * per_owner + jnp.sum(before, axis=1)
    first_seen = jnp.argmax(repeated, axis=1)
    fetch_at = jnp.where(leading, slot_of, slot_of[first_seen])
    target = jnp.where(leading, slot_of, devices * per_owner)
    requests = (
        jnp.full((devices * per_owner,), -1, jnp.int32).at[target].set(local_block, mode="drop")
    )
    wanted = lax.all_to_all(
        requests.reshape(devices, per_owner), "ctx", split_axis=0, concat_axis=0, tiled=True
    )
    chosen = jnp.maximum(wanted, 0)
    out_keys = key_blocks[chosen].reshape(devices, per_owner, SEL_BLOCK * DK)
    out_values = value_blocks[chosen].reshape(devices, per_owner, SEL_BLOCK * DV)
    got_keys, got_values = (
        lax.all_to_all(out_keys, "ctx", split_axis=0, concat_axis=0, tiled=True),
        lax.all_to_all(out_values, "ctx", split_axis=0, concat_axis=0, tiled=True),
    )
    near_keys = got_keys.reshape(devices * per_owner, SEL_BLOCK, DK)[fetch_at]
    near_values = got_values.reshape(devices * per_owner, SEL_BLOCK, DV)[fetch_at]
    own_index = cached * per_block + jnp.arange(groups, dtype=jnp.int32) * QBLOCK // SEL_BLOCK
    block_keys = jnp.concatenate(
        [key_blocks[own_index][:, None], near_keys.reshape(groups, listed - 1, SEL_BLOCK, DK)],
        axis=1,
    )
    block_values = jnp.concatenate(
        [value_blocks[own_index][:, None], near_values.reshape(groups, listed - 1, SEL_BLOCK, DV)],
        axis=1,
    )
    key_count = listed * SEL_BLOCK
    block_keys = block_keys.reshape(groups, key_count, DK)
    block_values = block_values.reshape(groups, key_count, DV)
    own_pos = (own_index - cached * per_block)[:, None] * SEL_BLOCK + jnp.arange(
        SEL_BLOCK, dtype=jnp.int32
    )[None, :]
    query_off = (
        jnp.arange(groups, dtype=jnp.int32)[:, None] * QBLOCK
        + jnp.arange(QBLOCK, dtype=jnp.int32)[None, :]
    )
    own_allowed = own_pos[:, None, :] <= query_off[:, :, None]
    far_allowed = jnp.repeat(usable.reshape(groups, listed - 1), SEL_BLOCK, axis=1)
    allowed = jnp.concatenate(
        [
            own_allowed,
            jnp.broadcast_to(far_allowed[:, None, :], (groups, QBLOCK, (listed - 1) * SEL_BLOCK)),
        ],
        axis=2,
    )
    grouped_q = queries.reshape(groups, QBLOCK * HEADS, DK)
    scores = (
        jnp.einsum("aqd,akd->aqk", grouped_q, block_keys, preferred_element_type=jnp.float32)
        * scaling
    )
    scores = jnp.where(
        allowed[:, :, None, :], scores.reshape(groups, QBLOCK, HEADS, key_count), -jnp.inf
    )
    sel_highest = jnp.max(scores, axis=3, keepdims=True)
    weights = jnp.exp(scores - sel_highest)
    sel_totals = jnp.sum(weights, axis=3)
    mixture = jnp.einsum(
        "aqk,akd->aqd",
        weights.astype(jnp.bfloat16).reshape(groups, QBLOCK * HEADS, key_count),
        block_values,
        preferred_element_type=jnp.float32,
    )
    selected = mixture.reshape(tokens, HEADS, DV) / sel_totals.reshape(tokens, HEADS)[:, :, None]
    gate_values = jax.nn.sigmoid(gate_logits.astype(jnp.float32)).reshape(tokens, 3, HEADS)
    combined = (
        gate_values[:, 0, :, None] * compressed
        + gate_values[:, 1, :, None] * selected
        + gate_values[:, 2, :, None] * sliding
    )
    return combined.reshape(tokens, HEADS * DV).astype(jnp.bfloat16)


PAIR = 2
COMP_ROWS = 48
PIECE_ROWS = DK + DV
CACHED_ROWS = PIECE_ROWS + COMP_ROWS
HALF = 64
STEP_HEADS = 4
LOG2E = 1.4426950408889634


def pack_kernel(keys_t, values, gains_k, gains_v, mix_k, mix_v, message):
    rounds, _, tokens = keys_t.shape
    count = tokens // CMP_BLOCK
    pooled_k = jnp.zeros((DK, tokens), jnp.float32)
    lane = lax.broadcasted_iota(jnp.int32, (tokens, tokens), 1)
    segment = lax.broadcasted_iota(jnp.int32, (tokens, tokens), 0) // CMP_BLOCK
    pooled_v = []
    for piece in range(rounds):
        base = 0 if piece == 0 else CACHED_ROWS
        message[base : base + DK, :] = keys_t[piece]
        message[base + DK : base + PIECE_ROWS, :] = values[piece]
        product = keys_t[piece].astype(jnp.float32) * gains_k[...]
        upper = product.astype(jnp.bfloat16)
        lower = (product - upper.astype(jnp.float32)).astype(jnp.bfloat16)
        picks = (lane == segment + piece * count).astype(jnp.bfloat16)
        pooled_k += jnp.dot(upper, picks, preferred_element_type=jnp.float32)
        pooled_k += jnp.dot(lower, picks, preferred_element_type=jnp.float32)
        product_v = values[piece].astype(jnp.float32) * gains_v[...]
        pooled_v.append(jnp.sum(product_v.reshape(count, CMP_BLOCK, DV), axis=1))
    comp_k = lax.dot_general(
        pooled_k.astype(jnp.bfloat16),
        mix_k[...],
        (((0,), (0,)), ((), ())),
        preferred_element_type=jnp.float32,
    )[: rounds * count]
    comp_v = jnp.dot(
        jnp.concatenate(pooled_v, axis=0).astype(jnp.bfloat16),
        mix_v[...],
        preferred_element_type=jnp.float32,
    )
    gap = jnp.zeros((rounds * count, HALF), jnp.float32)
    low = jnp.concatenate([comp_k, gap], axis=1)
    high = jnp.concatenate([gap, comp_k], axis=1)
    rows = [low[:, :DV], low[:, DV:], high[:, :DV], high[:, DV:], comp_v]
    rows.append(jnp.zeros((COMP_ROWS - 5 * rounds * count, DV), jnp.float32))
    message[PIECE_ROWS:CACHED_ROWS, :] = jnp.concatenate(rows, axis=0).astype(jnp.bfloat16)


def softmax_parts(scores):
    highest = scores[0].max(axis=1, keepdims=True)
    for part in scores[1:]:
        highest = jnp.maximum(highest, part.max(axis=1, keepdims=True))
    factor = DK ** (-0.5) * LOG2E
    return [jnp.exp2((part - highest) * factor).astype(jnp.bfloat16) for part in scores]


def weighted(weights, values):
    mixed = jnp.dot(weights[0], values[0], preferred_element_type=jnp.float32)
    for weight, value in zip(weights[1:], values[1:]):
        mixed += jnp.dot(weight, value, preferred_element_type=jnp.float32)
    return mixed[:, :DV] / mixed[:, DV:]


def attend_kernel(
    where_from,
    queries,
    gates,
    sel_bias,
    cmp_bias,
    *rest,
):
    *messages, output, far_low, far_high, far_values, near_low, near_high, near_values = rest[:-4]
    comp_low, comp_high, comp_values, bias = rest[-4:]
    tokens = queries.shape[0]
    slots = len(messages)
    per_slot = 2 * tokens // CMP_BLOCK

    @pl.when(pl.program_id(0) == 0)
    def _():
        for low, high in ((far_low, far_high), (near_low, near_high)):
            nothing = jnp.zeros((HALF, low.shape[1]), jnp.bfloat16)
            low[DK:, :] = nothing
            high[:HALF, :] = nothing
        for ref in (far_values, near_values, comp_values):
            ref[:, DV:] = jnp.ones((ref.shape[0], DV), jnp.bfloat16)
        for slot, message in enumerate(messages):
            span = slice(slot * tokens, (slot + 1) * tokens)
            far_low[:DK, span] = message[:DK, :]
            far_high[HALF:, span] = message[:DK, :]
            far_values[span, :DV] = message[DK:PIECE_ROWS, :]
            rows = slice(slot * per_slot, (slot + 1) * per_slot)
            part = message[PIECE_ROWS:CACHED_ROWS, :].astype(jnp.float32)
            comp_low[rows, :DV] = part[:per_slot]
            comp_low[rows, DV:] = part[per_slot : 2 * per_slot]
            comp_high[rows, :DV] = part[2 * per_slot : 3 * per_slot]
            comp_high[rows, DV:] = part[3 * per_slot : 4 * per_slot]
            comp_values[rows, :DV] = part[4 * per_slot : 5 * per_slot].astype(jnp.bfloat16)
        for place in range(5):
            lanes = slice(place * tokens, (place + 1) * tokens)

            def fetch(message, start):
                part = message[pl.ds(start, PIECE_ROWS), :]
                near_low[:DK, lanes] = part[:DK]
                near_high[HALF:, lanes] = part[:DK]
                near_values[lanes, :DV] = part[DK:]

            if place == 4:
                fetch(messages[0], CACHED_ROWS)
                continue
            for slot, message in enumerate(messages):

                @pl.when(where_from[0, place] == slot)
                def _():
                    start = where_from[1, place] * CACHED_ROWS
                    fetch(message, pl.multiple_of(start, 16))

        groups = sel_bias.shape[0]
        width = sel_bias.shape[1]
        bias[...] = jnp.broadcast_to(
            sel_bias[...][:, None, :], (groups, tokens // groups, width)
        ).reshape(tokens, width)

    query = lax.broadcasted_iota(jnp.int32, (tokens, tokens), 0)
    place_at = lax.broadcasted_iota(jnp.int32, (tokens, tokens), 1)
    never = jnp.float32(-jnp.inf)
    causal = jnp.where(place_at <= query, 0.0, never)
    expiring = jnp.where(place_at > query, 0.0, never)
    own_block = jnp.where(
        (place_at <= query) & (place_at // SEL_BLOCK == query // SEL_BLOCK), 0.0, never
    )

    def add(scores, mask):
        width = scores.shape[1]
        shape = (scores.shape[0] // tokens, tokens, width)
        return (scores.reshape(shape) + mask[None]).reshape(scores.shape)

    gate = jax.nn.sigmoid(gates[0].astype(jnp.float32))
    for odd, far, near, comp in ((0, far_low, near_low, comp_low), (1, far_high, near_high, comp_high)):
        first = odd * DV
        stride = 2 * DK
        rows = jnp.concatenate(
            [queries[:, first : first + 2 * DV], queries[:, first + stride : first + stride + 2 * DV]],
            axis=0,
        )
        near_scores = jnp.dot(rows, near[...], preferred_element_type=jnp.float32)
        far_scores = jnp.dot(rows, far[...], preferred_element_type=jnp.float32)
        comp_scores = lax.dot_general(
            rows,
            comp[...].astype(jnp.bfloat16),
            (((1,), (1,)), ((), ())),
            preferred_element_type=jnp.float32,
        )
        own = near_scores[:, 4 * tokens :]
        sliding = weighted(
            softmax_parts(
                [
                    add(near_scores[:, :tokens], expiring),
                    near_scores[:, tokens : 4 * tokens],
                    add(own, causal),
                ]
            ),
            [
                near_values[:tokens, :],
                near_values[tokens : 4 * tokens, :],
                near_values[4 * tokens :, :],
            ],
        )
        selected = weighted(
            softmax_parts([add(far_scores, bias[...]), add(own, own_block)]),
            [far_values[...], near_values[4 * tokens :, :]],
        )
        compressed = weighted(softmax_parts([add(comp_scores, cmp_bias[...])]), [comp_values[...]])
        for which in range(2):
            head = 2 * which + odd
            at = slice(which * tokens, (which + 1) * tokens)
            total = (
                gate[:, head : head + 1] * compressed[at]
                + gate[:, STEP_HEADS + head : STEP_HEADS + head + 1] * selected[at]
                + gate[:, 2 * STEP_HEADS + head : 2 * STEP_HEADS + head + 1] * sliding[at]
            )
            output[:, head * DV : (head + 1) * DV] = total.astype(jnp.bfloat16)


def dense_body(queries, keys, values, gate_logits, sel_ids, pos_k, pos_v, mix_k, mix_v):
    devices = lax.axis_size("ctx")
    myself = lax.axis_index("ctx")
    tokens = keys.shape[1]
    groups = sel_ids.shape[0]
    majors = devices // PAIR
    repeat = tokens // CMP_BLOCK
    gains_k = jnp.tile(pos_k.T.astype(jnp.float32), (1, repeat))
    gains_v = jnp.tile(pos_v.astype(jnp.float32), (repeat, 1))
    rows = CACHED_ROWS + PIECE_ROWS
    message = pl.pallas_call(
        pack_kernel,
        out_shape=jax.ShapeDtypeStruct((rows, tokens), jnp.bfloat16),
        name="pack",
    )(jnp.swapaxes(keys, 1, 2), values, gains_k, gains_v, mix_k, mix_v)

    def flipped(value):
        return lax.ppermute(value, "ctx", [(i, i ^ 1) for i in range(devices)])

    moved = []
    for step in range(1, majors):
        sent = message if step <= 2 else message[:CACHED_ROWS]
        moved.append(shifted(sent, "ctx", step * PAIR))
    other = flipped(message)
    messages = [message, other]
    for value in moved:
        messages += [value, flipped(value)]
    major, side = myself // PAIR, myself % PAIR
    holders = []
    for step in range(majors):
        source = (major - step) % majors * PAIR
        holders += [source + side, source + 1 - side]
    holders = jnp.stack(holders).astype(jnp.int32)
    distance = jnp.array([4, 3, 2, 1], jnp.int32)
    piece = myself - distance
    slot = jnp.where(side == 0, jnp.array([4, 5, 2, 3]), jnp.array([4, 3, 2, 1]))
    where_from = jnp.stack([slot, (piece >= 0).astype(jnp.int32)]).astype(jnp.int32)
    per_block = tokens // SEL_BLOCK
    block_of = (holders[:, None] * per_block + jnp.arange(per_block, dtype=jnp.int32)).reshape(-1)
    named = jnp.any(sel_ids[:, 1:, None] == block_of[None, None, :], axis=1)
    sel_bias = jnp.repeat(jnp.where(named, 0.0, -jnp.inf), SEL_BLOCK, axis=1)
    offset = jnp.arange(tokens, dtype=jnp.int32)[:, None]
    ends = (jnp.arange(repeat, dtype=jnp.int32) + 1) * CMP_BLOCK - 1
    ready = jnp.where(holders[:, None] == myself, ends[None, :], jnp.where(holders[:, None] < myself, -1, tokens))
    ready = jnp.concatenate([jnp.full((devices, repeat), -1, jnp.int32), ready], axis=1).reshape(-1)
    cmp_bias = jnp.where(ready[None, :] <= offset, 0.0, -jnp.inf)
    steps = HEADS // STEP_HEADS
    gates = (
        gate_logits.reshape(tokens, 3, steps, STEP_HEADS)
        .transpose(2, 0, 1, 3)
        .reshape(steps, tokens, 3 * STEP_HEADS)
    )
    far = devices * tokens
    comps = devices * 2 * repeat
    whole = lambda value: pl.BlockSpec(value.shape, lambda i: (0,) * value.ndim)
    return pl.pallas_call(
        attend_kernel,
        grid=(steps,),
        in_specs=[
            pl.BlockSpec(memory_space=pltpu.SMEM),
            pl.BlockSpec((tokens, STEP_HEADS * DK), lambda i: (0, i)),
            pl.BlockSpec((1, tokens, 3 * STEP_HEADS), lambda i: (i, 0, 0)),
            whole(sel_bias),
            whole(cmp_bias),
        ]
        + [whole(value) for value in messages],
        out_specs=pl.BlockSpec((tokens, STEP_HEADS * DV), lambda i: (0, i)),
        out_shape=jax.ShapeDtypeStruct((tokens, HEADS * DV), jnp.bfloat16),
        scratch_shapes=[
            pltpu.VMEM((2 * DV, far), jnp.bfloat16),
            pltpu.VMEM((2 * DV, far), jnp.bfloat16),
            pltpu.VMEM((far, 2 * DV), jnp.bfloat16),
            pltpu.VMEM((2 * DV, 5 * tokens), jnp.bfloat16),
            pltpu.VMEM((2 * DV, 5 * tokens), jnp.bfloat16),
            pltpu.VMEM((5 * tokens, 2 * DV), jnp.bfloat16),
            pltpu.VMEM((comps, 2 * DV), jnp.float32),
            pltpu.VMEM((comps, 2 * DV), jnp.float32),
            pltpu.VMEM((comps, 2 * DV), jnp.bfloat16),
            pltpu.VMEM((tokens, far), jnp.float32),
        ],
        name="attend",
    )(where_from, queries, gates, sel_bias, cmp_bias, *messages)


def body(queries, keys, *others):
    devices = lax.axis_size("ctx")
    rounds, tokens = keys.shape[:2]
    blocks = (rounds - 1) * tokens // SEL_BLOCK * devices
    dense = rounds == 2 and blocks <= SPREAD and devices % PAIR == 0 and devices >= 6
    chosen = dense_body if dense else exchange_body
    return chosen(queries, keys, *others)


def solution(mesh):
    in_specs = (
        P("ctx", "grp"),
        P(None, "ctx", "grp"),
        P(None, "ctx", "grp"),
        P("ctx", "grp"),
        P("ctx", "grp"),
        P(None, "grp"),
        P(None, "grp"),
        P(None, "grp"),
        P(None, "grp"),
    )
    out_specs = P("ctx", "grp")
    return jax.shard_map(body, mesh=mesh, in_specs=in_specs, out_specs=out_specs, check_vma=False)
```

```python
import functools

import jax
import jax.numpy as jnp
from jax import lax
from jax.experimental import pallas as pl
from jax.experimental.pallas import tpu as pltpu
from jax.sharding import PartitionSpec as P

HEADS = 16
DK = 192
DV = 128
CMP_BLOCK = 32
SEL_BLOCK = 64
QBLOCK = 16
SPREAD = 64


def shifted(value, axis, steps):
    count = lax.axis_size(axis)
    pairs = [(source, (source + steps) % count) for source in range(count)]
    return lax.ppermute(value, axis, pairs)


def attention(query_rows, key_rows, value_rows, allowed, head_count):
    scores = jnp.dot(query_rows, key_rows.T, preferred_element_type=jnp.float32) * query_rows.shape[
        1
    ] ** (-0.5)
    scores = scores.reshape(-1, head_count, key_rows.shape[0])
    scores = jnp.where(allowed[:, None, :], scores, -jnp.inf)
    highest = jnp.max(scores, axis=2, keepdims=True)
    weights = jnp.exp(scores - highest)
    totals = jnp.sum(weights, axis=2)
    rounded = weights.astype(jnp.bfloat16).reshape(-1, key_rows.shape[0])
    mixture = jnp.dot(rounded, value_rows, preferred_element_type=jnp.float32)
    return mixture.reshape(-1, head_count, value_rows.shape[1]) / totals[:, :, None]


def exchange_body(queries, keys, values, gate_logits, sel_ids, pos_k, pos_v, mix_k, mix_v):
    devices = lax.axis_size("ctx")
    myself = lax.axis_index("ctx")
    rounds = keys.shape[0]
    cached = rounds - 1
    tokens = keys.shape[1]
    scaling = DK ** (-0.5)
    query_rows = queries.reshape(tokens * HEADS, DK)
    query_pos = (cached * devices + myself) * tokens + jnp.arange(tokens, dtype=jnp.int32)
    paired = jnp.concatenate([keys, values], axis=2)
    earlier_rows = []
    for shift_by in range(1, 5):
        wrapped = myself + shift_by >= devices
        outgoing = jnp.where(wrapped, paired[0], paired[1])
        earlier_rows.append(shifted(outgoing, "ctx", shift_by))
    per_piece = tokens // CMP_BLOCK
    local_count = rounds * per_piece
    pooled_k = jnp.einsum(
        "bjd,jd->bd",
        keys.reshape(local_count, CMP_BLOCK, DK),
        pos_k,
        preferred_element_type=jnp.float32,
    ).astype(jnp.bfloat16)
    pooled_v = jnp.einsum(
        "bjd,jd->bd",
        values.reshape(local_count, CMP_BLOCK, DV),
        pos_v,
        preferred_element_type=jnp.float32,
    ).astype(jnp.bfloat16)
    comp_keys = jnp.dot(pooled_k, mix_k, preferred_element_type=jnp.float32).astype(jnp.bfloat16)
    comp_values = jnp.dot(pooled_v, mix_v, preferred_element_type=jnp.float32).astype(jnp.bfloat16)
    all_keys, all_values = (
        lax.all_gather(comp_keys, "ctx", axis=0, tiled=True),
        lax.all_gather(comp_values, "ctx", axis=0, tiled=True),
    )
    length = all_keys.shape[0]
    summed = jnp.zeros((tokens, HEADS, DV), jnp.float32)
    highest = jnp.full((tokens, HEADS), -jnp.inf, jnp.float32)
    totals = jnp.zeros((tokens, HEADS), jnp.float32)
    for low_row in range(0, length, 512):
        high_row = min(length, low_row + 512)
        key_index = low_row + jnp.arange(high_row - low_row, dtype=jnp.int32)
        holder = key_index // local_count
        within = key_index % local_count
        end_pos = (
            (within // per_piece * devices + holder) * tokens
            + (within % per_piece + 1) * CMP_BLOCK
            - 1
        )
        allowed = end_pos[None, :] <= query_pos[:, None]
        scores = (
            jnp.dot(query_rows, all_keys[low_row:high_row].T, preferred_element_type=jnp.float32)
            * scaling
        )
        scores = jnp.where(
            allowed[:, None, :], scores.reshape(tokens, HEADS, high_row - low_row), -jnp.inf
        )
        raised = jnp.maximum(highest, jnp.max(scores, axis=2))
        anchor = jnp.where(raised == -jnp.inf, 0.0, raised)
        weights = jnp.exp(scores - anchor[:, :, None])
        factor = jnp.exp(highest - anchor)
        totals = totals * factor + jnp.sum(weights, axis=2)
        mixture = jnp.dot(
            weights.astype(jnp.bfloat16).reshape(tokens * HEADS, high_row - low_row),
            all_values[low_row:high_row],
            preferred_element_type=jnp.float32,
        )
        summed = summed * factor[:, :, None] + mixture.reshape(tokens, HEADS, DV)
        highest = raised
    compressed = summed / totals[:, :, None]
    window_rows = jnp.concatenate(earlier_rows[::-1] + [paired[1]], axis=0)
    column = jnp.arange(5 * tokens, dtype=jnp.int32)[None, :]
    offsets = jnp.arange(tokens, dtype=jnp.int32)[:, None]
    inside = (column > offsets) & (column <= 4 * tokens + offsets)
    sliding = attention(query_rows, window_rows[:, :DK], window_rows[:, DK:], inside, HEADS)
    per_block = tokens // SEL_BLOCK
    groups = sel_ids.shape[0]
    listed = sel_ids.shape[1]
    remote = sel_ids[:, 1:].reshape(-1)
    entries = remote.shape[0]
    usable = remote >= 0
    clipped = jnp.maximum(remote, 0)
    holder_piece = clipped // per_block
    holder = holder_piece % devices
    local_block = holder_piece // devices * per_block + clipped % per_block
    distinct = min(SPREAD, cached * per_block * devices)
    per_owner = -(-distinct // devices)
    earlier = jnp.arange(entries)[None, :] < jnp.arange(entries)[:, None]
    same_owner = holder[:, None] == holder[None, :]
    key_blocks = keys.reshape(rounds * per_block, SEL_BLOCK, DK)
    value_blocks = values.reshape(rounds * per_block, SEL_BLOCK, DV)
    repeated = (remote[:, None] == remote[None, :]) & usable[None, :] & earlier
    leading = usable & ~jnp.any(repeated, axis=1)
    before = same_owner & leading[None, :] & earlier
    slot_of = holder * per_owner + jnp.sum(before, axis=1)
    first_seen = jnp.argmax(repeated, axis=1)
    fetch_at = jnp.where(leading, slot_of, slot_of[first_seen])
    target = jnp.where(leading, slot_of, devices * per_owner)
    requests = (
        jnp.full((devices * per_owner,), -1, jnp.int32).at[target].set(local_block, mode="drop")
    )
    wanted = lax.all_to_all(
        requests.reshape(devices, per_owner), "ctx", split_axis=0, concat_axis=0, tiled=True
    )
    chosen = jnp.maximum(wanted, 0)
    out_keys = key_blocks[chosen].reshape(devices, per_owner, SEL_BLOCK * DK)
    out_values = value_blocks[chosen].reshape(devices, per_owner, SEL_BLOCK * DV)
    got_keys, got_values = (
        lax.all_to_all(out_keys, "ctx", split_axis=0, concat_axis=0, tiled=True),
        lax.all_to_all(out_values, "ctx", split_axis=0, concat_axis=0, tiled=True),
    )
    near_keys = got_keys.reshape(devices * per_owner, SEL_BLOCK, DK)[fetch_at]
    near_values = got_values.reshape(devices * per_owner, SEL_BLOCK, DV)[fetch_at]
    own_index = cached * per_block + jnp.arange(groups, dtype=jnp.int32) * QBLOCK // SEL_BLOCK
    block_keys = jnp.concatenate(
        [key_blocks[own_index][:, None], near_keys.reshape(groups, listed - 1, SEL_BLOCK, DK)],
        axis=1,
    )
    block_values = jnp.concatenate(
        [value_blocks[own_index][:, None], near_values.reshape(groups, listed - 1, SEL_BLOCK, DV)],
        axis=1,
    )
    key_count = listed * SEL_BLOCK
    block_keys = block_keys.reshape(groups, key_count, DK)
    block_values = block_values.reshape(groups, key_count, DV)
    own_pos = (own_index - cached * per_block)[:, None] * SEL_BLOCK + jnp.arange(
        SEL_BLOCK, dtype=jnp.int32
    )[None, :]
    query_off = (
        jnp.arange(groups, dtype=jnp.int32)[:, None] * QBLOCK
        + jnp.arange(QBLOCK, dtype=jnp.int32)[None, :]
    )
    own_allowed = own_pos[:, None, :] <= query_off[:, :, None]
    far_allowed = jnp.repeat(usable.reshape(groups, listed - 1), SEL_BLOCK, axis=1)
    allowed = jnp.concatenate(
        [
            own_allowed,
            jnp.broadcast_to(far_allowed[:, None, :], (groups, QBLOCK, (listed - 1) * SEL_BLOCK)),
        ],
        axis=2,
    )
    grouped_q = queries.reshape(groups, QBLOCK * HEADS, DK)
    scores = (
        jnp.einsum("aqd,akd->aqk", grouped_q, block_keys, preferred_element_type=jnp.float32)
        * scaling
    )
    scores = jnp.where(
        allowed[:, :, None, :], scores.reshape(groups, QBLOCK, HEADS, key_count), -jnp.inf
    )
    sel_highest = jnp.max(scores, axis=3, keepdims=True)
    weights = jnp.exp(scores - sel_highest)
    sel_totals = jnp.sum(weights, axis=3)
    mixture = jnp.einsum(
        "aqk,akd->aqd",
        weights.astype(jnp.bfloat16).reshape(groups, QBLOCK * HEADS, key_count),
        block_values,
        preferred_element_type=jnp.float32,
    )
    selected = mixture.reshape(tokens, HEADS, DV) / sel_totals.reshape(tokens, HEADS)[:, :, None]
    gate_values = jax.nn.sigmoid(gate_logits.astype(jnp.float32)).reshape(tokens, 3, HEADS)
    combined = (
        gate_values[:, 0, :, None] * compressed
        + gate_values[:, 1, :, None] * selected
        + gate_values[:, 2, :, None] * sliding
    )
    return combined.reshape(tokens, HEADS * DV).astype(jnp.bfloat16)


PAIR = 2
COMP_ROWS = 32
PIECE_ROWS = DK + DV
CACHED_ROWS = COMP_ROWS + PIECE_ROWS
HALF = 64
NEAR = 4
NEAR_SLOTS = ((4, 4), (5, 3), (2, 2), (3, 1))
BASE2_SCALE = DK ** (-0.5) * 1.4426950408889634
NEVER = -jnp.inf
KERNEL_PARAMS = pltpu.CompilerParams(vmem_limit_bytes=32 * 2**20)


def pack_kernel(keys_t, values, pos_k, pos_v, mix_k, mix_v, whole, cached):
    rounds, _, tokens = keys_t.shape
    count = tokens // CMP_BLOCK
    gains_k = jnp.concatenate([pos_k[...].astype(jnp.float32)] * count, axis=0).T
    gains_v = jnp.concatenate([pos_v[...].astype(jnp.float32)] * count, axis=0)
    pooled_k = jnp.zeros((DK, tokens), jnp.float32)
    lane = lax.broadcasted_iota(jnp.int32, (tokens, tokens), 1)
    segment = lax.broadcasted_iota(jnp.int32, (tokens, tokens), 0) // CMP_BLOCK
    pooled_v = []
    for piece in range(rounds):
        base = COMP_ROWS + piece * PIECE_ROWS
        for out in (whole, cached)[: 2 - piece]:
            out[base : base + DK, :] = keys_t[piece]
            out[base + DK : base + PIECE_ROWS, :] = values[piece]
        product = keys_t[piece].astype(jnp.float32) * gains_k
        upper = product.astype(jnp.bfloat16)
        lower = (product - upper.astype(jnp.float32)).astype(jnp.bfloat16)
        picks = (lane == segment + piece * count).astype(jnp.bfloat16)
        pooled_k += jnp.dot(upper, picks, preferred_element_type=jnp.float32)
        pooled_k += jnp.dot(lower, picks, preferred_element_type=jnp.float32)
        product_v = values[piece].astype(jnp.float32) * gains_v
        pooled_v.append(jnp.sum(product_v.reshape(count, CMP_BLOCK, DV), axis=1))
    comp_k = lax.dot_general(
        pooled_k.astype(jnp.bfloat16),
        mix_k[...],
        (((0,), (0,)), ((), ())),
        preferred_element_type=jnp.float32,
    )[: rounds * count]
    comp_v = jnp.dot(
        jnp.concatenate(pooled_v, axis=0).astype(jnp.bfloat16),
        mix_v[...],
        preferred_element_type=jnp.float32,
    )
    comp_k = jnp.concatenate([comp_k, jnp.zeros((rounds * count, HALF), jnp.float32)], axis=1)
    rows = [comp_k[:, :DV], comp_k[:, DV:], comp_v]
    rows.append(jnp.zeros((COMP_ROWS - 3 * rounds * count, DV), jnp.float32))
    packed = jnp.concatenate(rows, axis=0).astype(jnp.bfloat16)
    whole[:COMP_ROWS, :] = packed
    cached[:COMP_ROWS, :] = packed


def holder_of(slot, myself, devices):
    source = lax.rem(myself // PAIR - slot // PAIR + devices // PAIR, devices // PAIR) * PAIR
    side = lax.rem(myself, PAIR)
    return source + (side if slot % PAIR == 0 else 1 - side)


def add(scores, mask):
    shape = (scores.shape[0] // mask.shape[0],) + mask.shape
    return (scores.reshape(shape) + mask[None]).reshape(scores.shape)


def prepare_kernel(devices, me_ref, gate_ref, sel_ref, gate_wide, bias, comp_bias):
    groups = sel_ref.shape[0]
    tokens = groups * QBLOCK
    per_slot = 2 * tokens // CMP_BLOCK
    myself = me_ref[0]
    gates = jax.nn.sigmoid(gate_ref[...].astype(jnp.float32))
    pad = jnp.zeros((2 * HALF - 3 * HEADS, tokens), jnp.float32)
    gates = jnp.concatenate([gates, pad], axis=0).T
    for column in range(3 * HEADS):
        spread = jnp.broadcast_to(gates[:, column : column + 1], (tokens, DV))
        gate_wide[:, column * DV : (column + 1) * DV] = spread
    ids = sel_ref[...]
    entry = lax.broadcasted_iota(jnp.int32, ids.shape, 1)
    lane = lax.broadcasted_iota(jnp.int32, (groups, tokens), 1)
    for slot in range(devices):
        first = holder_of(slot, myself, devices) * (tokens // SEL_BLOCK)
        row = jnp.full((groups, tokens), NEVER, jnp.float32)
        for block in range(tokens // SEL_BLOCK):
            found = jnp.where((ids == first + block) & (entry > 0), 1, 0)
            named = jnp.max(found, axis=1, keepdims=True) > 0
            row = jnp.where((lane // SEL_BLOCK == block) & named, 0.0, row)
        spread = jnp.broadcast_to(row[:, None, :], (groups, QBLOCK, tokens))
        bias[slot] = spread.reshape(tokens, tokens)
    query = lax.broadcasted_iota(jnp.int32, (tokens, tokens), 0)
    key_at = lax.broadcasted_iota(jnp.int32, (tokens, tokens), 1)
    same = key_at // SEL_BLOCK == query // SEL_BLOCK
    bias[devices] = jnp.where((key_at <= query) & same, 0.0, NEVER)
    column = lax.broadcasted_iota(jnp.int32, comp_bias.shape, 1)
    offset = lax.broadcasted_iota(jnp.int32, comp_bias.shape, 0)
    within = lax.rem(column, per_slot) - per_slot // 2
    ready = jnp.full(column.shape, -1, jnp.int32)
    for slot in range(devices):
        holder = holder_of(slot, myself, devices)
        late = jnp.where(holder > myself, tokens, -1)
        end = jnp.where(holder == myself, (within + 1) * CMP_BLOCK - 1, late)
        ready = jnp.where((column // per_slot == slot) & (within >= 0), end, ready)
    comp_bias[...] = jnp.where(ready <= offset, 0.0, NEVER)


def attend_call(devices, slots, args, carried, messages):
    me, queries, gate_wide, masks, comp_mask = args
    first_pass = carried is None
    tokens = queries.shape[0]
    per_slot = 2 * tokens // CMP_BLOCK
    near_width = (NEAR + 1) * tokens
    far_width = (len(slots) + first_pass) * tokens
    numbers = sorted(set(slots) | {0} if first_pass else messages)
    step_heads, unit_heads, lag = (8, 2, 2) if first_pass else (8, 2, 1)
    steps = HEADS // step_heads

    def kernel(*refs):
        refs = list(refs)
        me_ref, q_ref, mask_ref = refs[:3]
        del refs[:3]
        gate_ref, comp_bias = (None, None) if first_pass else (refs.pop(0), refs.pop(0))
        state = None if first_pass else [refs.pop(0) for _ in range(2)]
        pieces = {slot: refs.pop(0) for slot in numbers}
        outs = [refs.pop(0) for _ in range(2 if first_pass else 1)]
        far_low, far_high, far_values = refs[:3]
        if not first_pass:
            near_low, near_high, near_values, comp_low, comp_high, comp_values = refs[3:]
        tables = [(far_low, far_high, far_values)]
        tables += [] if first_pass else [(near_low, near_high, near_values)]
        myself = me_ref[0]
        query = lax.broadcasted_iota(jnp.int32, (tokens, tokens), 0)
        key_at = lax.broadcasted_iota(jnp.int32, (tokens, tokens), 1)

        def stage(table, at, piece, start):
            low, high, value = tables[table]
            lanes = slice(at * tokens, (at + 1) * tokens)
            part = piece[pl.ds(start, PIECE_ROWS), :]
            low[:DK, lanes] = part[:DK]
            high[HALF:, lanes] = part[:DK]
            value[lanes, :DV] = part[DK:]

        @pl.when(pl.program_id(0) == 0)
        def _():
            for low, high, value in tables:
                nothing = jnp.zeros((HALF, low.shape[1]), jnp.bfloat16)
                low[DK:, :] = nothing
                high[:HALF, :] = nothing
                value[:, DV:] = jnp.ones((value.shape[0], DV), jnp.bfloat16)
            for at, slot in enumerate(slots):
                stage(0, at, pieces[slot], COMP_ROWS)
            if first_pass:
                stage(0, len(slots), pieces[0], CACHED_ROWS)
                return
            side = lax.rem(myself, PAIR)
            for place, choices in enumerate(NEAR_SLOTS):
                in_span = (myself - (NEAR - place) >= 0).astype(jnp.int32)
                start = pl.multiple_of(COMP_ROWS + in_span * PIECE_ROWS, 16)
                if choices[0] == choices[1]:
                    stage(1, place, pieces[choices[0]], start)
                else:
                    for value, slot in enumerate(choices):
                        pl.when(side == value)(
                            lambda place=place, slot=slot, start=start: stage(
                                1, place, pieces[slot], start
                            )
                        )
            stage(1, NEAR, pieces[0], CACHED_ROWS)
            comp_values[:, DV:] = jnp.ones((devices * per_slot, DV), jnp.bfloat16)
            for slot in numbers:
                rows = slice(slot * per_slot, (slot + 1) * per_slot)
                part = pieces[slot][:COMP_ROWS, :].astype(jnp.float32)
                both = jnp.concatenate([part[:per_slot], part[per_slot : 2 * per_slot]], axis=1)
                comp_low[rows, :] = both
                comp_high[rows, :] = pltpu.roll(both, HALF, 1)
                comp_values[rows, :DV] = part[2 * per_slot : 3 * per_slot].astype(jnp.bfloat16)

        def gathered(ref, heads):
            return jnp.concatenate([ref[:, h * DV : (h + 1) * DV] for h in heads], axis=0)

        def score(odd, heads, kind):
            rows = jnp.concatenate(
                [q_ref[:, h * DK - odd * HALF : h * DK - odd * HALF + 2 * DV] for h in heads],
                axis=0,
            )
            if kind == "far":
                table = far_high if odd else far_low
                scores = jnp.dot(rows, table[...], preferred_element_type=jnp.float32)
                masks_of = list(slots) + [devices] * first_pass
                bias = jnp.concatenate([mask_ref[slot] for slot in masks_of], axis=1)
                return [add(scores, bias)]
            if kind == "comp":
                table = (comp_high if odd else comp_low)[...].astype(jnp.bfloat16)
                scores = lax.dot_general(
                    rows, table, (((1,), (1,)), ((), ())), preferred_element_type=jnp.float32
                )
                return [add(scores, comp_bias[...])]
            table = near_high if odd else near_low
            scores = jnp.dot(rows, table[...], preferred_element_type=jnp.float32)
            return [
                add(scores[:, :tokens], jnp.where(key_at > query, 0.0, NEVER)),
                scores[:, tokens : NEAR * tokens],
                add(scores[:, NEAR * tokens :], jnp.where(key_at <= query, 0.0, NEVER)),
            ]

        def weigh(heads, kind, scores):
            highest = scores[0].max(axis=1, keepdims=True)
            for part in scores[1:]:
                highest = jnp.maximum(highest, part.max(axis=1, keepdims=True))
            if kind == "far":
                highest = jnp.broadcast_to(highest, (highest.shape[0], DV))
                if not first_pass:
                    highest = jnp.maximum(highest, gathered(state[1], heads))
                wide = jnp.concatenate([highest] * (scores[0].shape[1] // DV), axis=1)
            else:
                wide = highest
            weights = [jnp.exp2((part - wide) * BASE2_SCALE).astype(jnp.bfloat16) for part in scores]
            return highest, weights

        def mix(heads, kind, highest, weights):
            taken = jnp.concatenate(weights, axis=1) if len(weights) > 1 else weights[0]
            value = far_values if kind == "far" else near_values if kind == "near" else comp_values
            both = jnp.dot(taken, value[...], preferred_element_type=jnp.float32)
            mixed, total = both[:, :DV], both[:, DV:]
            if kind == "far" and not first_pass:
                fade = jnp.exp2((gathered(state[1], heads) - highest) * BASE2_SCALE)
                mixed, total = mixed + gathered(state[0], heads) * fade, total + fade
            if kind == "far" and first_pass:
                return mixed / total, highest + jnp.log(total) * DK**0.5
            return mixed / total

        kinds = ("far",) if first_pass else ("comp", "far", "near")
        units = []
        for odd in range(2):
            for first in range(odd, step_heads, unit_heads * 2):
                heads = list(range(first, first + 2 * unit_heads, 2))
                units += [(odd, heads, kind) for kind in kinds[::-1]]
        found, scored, weighed = {}, {}, {}
        for turn in range(len(units) + 2 * lag):
            if turn < len(units):
                scored[turn] = score(*units[turn])
            at = turn - lag
            if 0 <= at < len(units):
                weighed[at] = weigh(*units[at][1:], scored.pop(at))
            at = turn - 2 * lag
            if 0 <= at < len(units):
                _, heads, kind = units[at]
                found[kind] = mix(heads, kind, *weighed.pop(at))
                if len(found) < len(kinds):
                    continue
                for which, head in enumerate(heads):
                    lines = slice(which * tokens, (which + 1) * tokens)
                    cols = slice(head * DV, (head + 1) * DV)
                    if first_pass:
                        for out, part in zip(outs, found["far"]):
                            out[:, cols] = part[lines]
                        continue
                    total = 0.0
                    for b, kind in enumerate(kinds):
                        column = b * HEADS + head + step_heads * pl.program_id(0)
                        lanes = pl.ds(pl.multiple_of(column * DV, DV), DV)
                        total += gate_ref[:, lanes] * found[kind][lines]
                    outs[0][:, cols] = total.astype(jnp.bfloat16)
                found = {}

    in_vmem = pl.BlockSpec(memory_space=pltpu.VMEM)
    by_head = pl.BlockSpec((tokens, step_heads * DV), lambda i: (0, i))
    in_specs = [
        pl.BlockSpec(memory_space=pltpu.SMEM),
        pl.BlockSpec((tokens, step_heads * DK), lambda i: (0, i)),
        in_vmem,
    ]
    operands = [me, queries, masks]
    if not first_pass:
        in_specs += [in_vmem] * 2
        operands += [gate_wide, comp_mask]
    if not first_pass:
        in_specs += [by_head] * 2
        operands += carried
    for slot in numbers:
        in_specs.append(in_vmem)
        operands.append(pltpu.with_memory_space_constraint(messages[slot], pltpu.VMEM))
    scratch = [
        pltpu.VMEM((2 * DV, far_width), jnp.bfloat16),
        pltpu.VMEM((2 * DV, far_width), jnp.bfloat16),
        pltpu.VMEM((far_width, 2 * DV), jnp.bfloat16),
    ]
    if not first_pass:
        scratch += [
            pltpu.VMEM((2 * DV, near_width), jnp.bfloat16),
            pltpu.VMEM((2 * DV, near_width), jnp.bfloat16),
            pltpu.VMEM((near_width, 2 * DV), jnp.bfloat16),
            pltpu.VMEM((devices * per_slot, 2 * DV), jnp.float32),
            pltpu.VMEM((devices * per_slot, 2 * DV), jnp.float32),
            pltpu.VMEM((devices * per_slot, 2 * DV), jnp.bfloat16),
        ]
    partial = [jax.ShapeDtypeStruct((tokens, HEADS * DV), jnp.float32)] * 2
    columns = far_width if first_pass else far_width + near_width
    return pl.pallas_call(
        kernel,
        grid=(steps,),
        in_specs=in_specs,
        out_specs=[by_head] * 2 if first_pass else by_head,
        out_shape=partial if first_pass else jax.ShapeDtypeStruct((tokens, HEADS * DV), jnp.bfloat16),
        scratch_shapes=scratch,
        cost_estimate=pl.CostEstimate(
            flops=2 * tokens * HEADS * columns * (DK + DV),
            transcendentals=tokens * HEADS * columns,
            bytes_accessed=2 * queries.size,
        ),
        compiler_params=KERNEL_PARAMS,
    )(*operands)


EARLY = (0, 1, 2, 3, 4, 6)


def dense_body(queries, keys, values, gate_logits, sel_ids, pos_k, pos_v, mix_k, mix_v):
    devices = lax.axis_size("ctx")
    tokens = keys.shape[1]
    rows = CACHED_ROWS + PIECE_ROWS
    message, cached = pl.pallas_call(
        pack_kernel,
        out_shape=[
            jax.ShapeDtypeStruct((rows, tokens), jnp.bfloat16),
            jax.ShapeDtypeStruct((CACHED_ROWS, tokens), jnp.bfloat16),
        ],
        name="pack",
    )(jnp.swapaxes(keys, 1, 2), values, pos_k, pos_v, mix_k, mix_v)

    in_vmem = pl.BlockSpec(memory_space=pltpu.VMEM)
    messages = {0: message}
    for slot in range(2, devices, PAIR):
        sent = message if slot <= 4 else cached
        messages[slot] = shifted(sent, "ctx", slot)
    for slot in range(0, devices, PAIR):
        pairs = [(i, i ^ 1) for i in range(devices)]
        messages[slot + 1] = lax.ppermute(messages[slot], "ctx", pairs)
    me = lax.axis_index("ctx").astype(jnp.int32).reshape(1)
    prepared = pl.pallas_call(
        functools.partial(prepare_kernel, devices),
        in_specs=[pl.BlockSpec(memory_space=pltpu.SMEM)] + [in_vmem] * 2,
        out_specs=[in_vmem] * 3,
        out_shape=[
            pltpu.VMEM((tokens, 3 * HEADS * DV), jnp.float32),
            pltpu.VMEM((devices + 1, tokens, tokens), jnp.float32),
            pltpu.VMEM((tokens, devices * 2 * tokens // CMP_BLOCK), jnp.float32),
        ],
        name="prepare", compiler_params=KERNEL_PARAMS,
    )(me, gate_logits.T, sel_ids)
    args = (me, queries, *prepared)
    late = tuple(slot for slot in messages if slot not in EARLY)
    state = attend_call(devices, EARLY, args, None, messages)
    return attend_call(devices, sorted(late), args, state, messages)


def body(queries, keys, *others):
    devices = lax.axis_size("ctx")
    rounds, tokens = keys.shape[:2]
    blocks = (rounds - 1) * tokens // SEL_BLOCK * devices
    dense = rounds == 2 and blocks <= SPREAD and devices % PAIR == 0 and devices >= 6
    chosen = dense_body if dense else exchange_body
    return chosen(queries, keys, *others)


def solution(mesh):
    in_specs = (
        P("ctx", "grp"),
        P(None, "ctx", "grp"),
        P(None, "ctx", "grp"),
        P("ctx", "grp"),
        P("ctx", "grp"),
        P(None, "grp"),
        P(None, "grp"),
        P(None, "grp"),
        P(None, "grp"),
    )
    out_specs = P("ctx", "grp")
    return jax.shard_map(body, mesh=mesh, in_specs=in_specs, out_specs=out_specs, check_vma=False)
```

```python
import functools

import jax
import jax.numpy as jnp
from jax import lax
from jax.experimental import pallas as pl
from jax.experimental.pallas import tpu as pltpu
from jax.sharding import PartitionSpec as P

HEADS = 16
DK = 192
DV = 128
CMP_BLOCK = 32
SEL_BLOCK = 64
QBLOCK = 16
SPREAD = 64


def shifted(value, axis, steps):
    count = lax.axis_size(axis)
    pairs = [(source, (source + steps) % count) for source in range(count)]
    return lax.ppermute(value, axis, pairs)


def attention(query_rows, key_rows, value_rows, allowed, head_count):
    scores = jnp.dot(query_rows, key_rows.T, preferred_element_type=jnp.float32) * query_rows.shape[
        1
    ] ** (-0.5)
    scores = scores.reshape(-1, head_count, key_rows.shape[0])
    scores = jnp.where(allowed[:, None, :], scores, -jnp.inf)
    highest = jnp.max(scores, axis=2, keepdims=True)
    weights = jnp.exp(scores - highest)
    totals = jnp.sum(weights, axis=2)
    rounded = weights.astype(jnp.bfloat16).reshape(-1, key_rows.shape[0])
    mixture = jnp.dot(rounded, value_rows, preferred_element_type=jnp.float32)
    return mixture.reshape(-1, head_count, value_rows.shape[1]) / totals[:, :, None]


def exchange_body(queries, keys, values, gate_logits, sel_ids, pos_k, pos_v, mix_k, mix_v):
    devices = lax.axis_size("ctx")
    myself = lax.axis_index("ctx")
    rounds = keys.shape[0]
    cached = rounds - 1
    tokens = keys.shape[1]
    scaling = DK ** (-0.5)
    query_rows = queries.reshape(tokens * HEADS, DK)
    query_pos = (cached * devices + myself) * tokens + jnp.arange(tokens, dtype=jnp.int32)
    paired = jnp.concatenate([keys, values], axis=2)
    earlier_rows = []
    for shift_by in range(1, 5):
        wrapped = myself + shift_by >= devices
        outgoing = jnp.where(wrapped, paired[0], paired[1])
        earlier_rows.append(shifted(outgoing, "ctx", shift_by))
    per_piece = tokens // CMP_BLOCK
    local_count = rounds * per_piece
    pooled_k = jnp.einsum(
        "bjd,jd->bd",
        keys.reshape(local_count, CMP_BLOCK, DK),
        pos_k,
        preferred_element_type=jnp.float32,
    ).astype(jnp.bfloat16)
    pooled_v = jnp.einsum(
        "bjd,jd->bd",
        values.reshape(local_count, CMP_BLOCK, DV),
        pos_v,
        preferred_element_type=jnp.float32,
    ).astype(jnp.bfloat16)
    comp_keys = jnp.dot(pooled_k, mix_k, preferred_element_type=jnp.float32).astype(jnp.bfloat16)
    comp_values = jnp.dot(pooled_v, mix_v, preferred_element_type=jnp.float32).astype(jnp.bfloat16)
    all_keys, all_values = (
        lax.all_gather(comp_keys, "ctx", axis=0, tiled=True),
        lax.all_gather(comp_values, "ctx", axis=0, tiled=True),
    )
    length = all_keys.shape[0]
    summed = jnp.zeros((tokens, HEADS, DV), jnp.float32)
    highest = jnp.full((tokens, HEADS), -jnp.inf, jnp.float32)
    totals = jnp.zeros((tokens, HEADS), jnp.float32)
    for low_row in range(0, length, 512):
        high_row = min(length, low_row + 512)
        key_index = low_row + jnp.arange(high_row - low_row, dtype=jnp.int32)
        holder = key_index // local_count
        within = key_index % local_count
        end_pos = (
            (within // per_piece * devices + holder) * tokens
            + (within % per_piece + 1) * CMP_BLOCK
            - 1
        )
        allowed = end_pos[None, :] <= query_pos[:, None]
        scores = (
            jnp.dot(query_rows, all_keys[low_row:high_row].T, preferred_element_type=jnp.float32)
            * scaling
        )
        scores = jnp.where(
            allowed[:, None, :], scores.reshape(tokens, HEADS, high_row - low_row), -jnp.inf
        )
        raised = jnp.maximum(highest, jnp.max(scores, axis=2))
        anchor = jnp.where(raised == -jnp.inf, 0.0, raised)
        weights = jnp.exp(scores - anchor[:, :, None])
        factor = jnp.exp(highest - anchor)
        totals = totals * factor + jnp.sum(weights, axis=2)
        mixture = jnp.dot(
            weights.astype(jnp.bfloat16).reshape(tokens * HEADS, high_row - low_row),
            all_values[low_row:high_row],
            preferred_element_type=jnp.float32,
        )
        summed = summed * factor[:, :, None] + mixture.reshape(tokens, HEADS, DV)
        highest = raised
    compressed = summed / totals[:, :, None]
    window_rows = jnp.concatenate(earlier_rows[::-1] + [paired[1]], axis=0)
    column = jnp.arange(5 * tokens, dtype=jnp.int32)[None, :]
    offsets = jnp.arange(tokens, dtype=jnp.int32)[:, None]
    inside = (column > offsets) & (column <= 4 * tokens + offsets)
    sliding = attention(query_rows, window_rows[:, :DK], window_rows[:, DK:], inside, HEADS)
    per_block = tokens // SEL_BLOCK
    groups = sel_ids.shape[0]
    listed = sel_ids.shape[1]
    remote = sel_ids[:, 1:].reshape(-1)
    entries = remote.shape[0]
    usable = remote >= 0
    clipped = jnp.maximum(remote, 0)
    holder_piece = clipped // per_block
    holder = holder_piece % devices
    local_block = holder_piece // devices * per_block + clipped % per_block
    distinct = min(SPREAD, cached * per_block * devices)
    per_owner = -(-distinct // devices)
    earlier = jnp.arange(entries)[None, :] < jnp.arange(entries)[:, None]
    same_owner = holder[:, None] == holder[None, :]
    key_blocks = keys.reshape(rounds * per_block, SEL_BLOCK, DK)
    value_blocks = values.reshape(rounds * per_block, SEL_BLOCK, DV)
    repeated = (remote[:, None] == remote[None, :]) & usable[None, :] & earlier
    leading = usable & ~jnp.any(repeated, axis=1)
    before = same_owner & leading[None, :] & earlier
    slot_of = holder * per_owner + jnp.sum(before, axis=1)
    first_seen = jnp.argmax(repeated, axis=1)
    fetch_at = jnp.where(leading, slot_of, slot_of[first_seen])
    target = jnp.where(leading, slot_of, devices * per_owner)
    requests = (
        jnp.full((devices * per_owner,), -1, jnp.int32).at[target].set(local_block, mode="drop")
    )
    wanted = lax.all_to_all(
        requests.reshape(devices, per_owner), "ctx", split_axis=0, concat_axis=0, tiled=True
    )
    chosen = jnp.maximum(wanted, 0)
    out_keys = key_blocks[chosen].reshape(devices, per_owner, SEL_BLOCK * DK)
    out_values = value_blocks[chosen].reshape(devices, per_owner, SEL_BLOCK * DV)
    got_keys, got_values = (
        lax.all_to_all(out_keys, "ctx", split_axis=0, concat_axis=0, tiled=True),
        lax.all_to_all(out_values, "ctx", split_axis=0, concat_axis=0, tiled=True),
    )
    near_keys = got_keys.reshape(devices * per_owner, SEL_BLOCK, DK)[fetch_at]
    near_values = got_values.reshape(devices * per_owner, SEL_BLOCK, DV)[fetch_at]
    own_index = cached * per_block + jnp.arange(groups, dtype=jnp.int32) * QBLOCK // SEL_BLOCK
    block_keys = jnp.concatenate(
        [key_blocks[own_index][:, None], near_keys.reshape(groups, listed - 1, SEL_BLOCK, DK)],
        axis=1,
    )
    block_values = jnp.concatenate(
        [value_blocks[own_index][:, None], near_values.reshape(groups, listed - 1, SEL_BLOCK, DV)],
        axis=1,
    )
    key_count = listed * SEL_BLOCK
    block_keys = block_keys.reshape(groups, key_count, DK)
    block_values = block_values.reshape(groups, key_count, DV)
    own_pos = (own_index - cached * per_block)[:, None] * SEL_BLOCK + jnp.arange(
        SEL_BLOCK, dtype=jnp.int32
    )[None, :]
    query_off = (
        jnp.arange(groups, dtype=jnp.int32)[:, None] * QBLOCK
        + jnp.arange(QBLOCK, dtype=jnp.int32)[None, :]
    )
    own_allowed = own_pos[:, None, :] <= query_off[:, :, None]
    far_allowed = jnp.repeat(usable.reshape(groups, listed - 1), SEL_BLOCK, axis=1)
    allowed = jnp.concatenate(
        [
            own_allowed,
            jnp.broadcast_to(far_allowed[:, None, :], (groups, QBLOCK, (listed - 1) * SEL_BLOCK)),
        ],
        axis=2,
    )
    grouped_q = queries.reshape(groups, QBLOCK * HEADS, DK)
    scores = (
        jnp.einsum("aqd,akd->aqk", grouped_q, block_keys, preferred_element_type=jnp.float32)
        * scaling
    )
    scores = jnp.where(
        allowed[:, :, None, :], scores.reshape(groups, QBLOCK, HEADS, key_count), -jnp.inf
    )
    sel_highest = jnp.max(scores, axis=3, keepdims=True)
    weights = jnp.exp(scores - sel_highest)
    sel_totals = jnp.sum(weights, axis=3)
    mixture = jnp.einsum(
        "aqk,akd->aqd",
        weights.astype(jnp.bfloat16).reshape(groups, QBLOCK * HEADS, key_count),
        block_values,
        preferred_element_type=jnp.float32,
    )
    selected = mixture.reshape(tokens, HEADS, DV) / sel_totals.reshape(tokens, HEADS)[:, :, None]
    gate_values = jax.nn.sigmoid(gate_logits.astype(jnp.float32)).reshape(tokens, 3, HEADS)
    combined = (
        gate_values[:, 0, :, None] * compressed
        + gate_values[:, 1, :, None] * selected
        + gate_values[:, 2, :, None] * sliding
    )
    return combined.reshape(tokens, HEADS * DV).astype(jnp.bfloat16)


PAIR = 2
COMP_ROWS = 32
PIECE_ROWS = DK + DV
CACHED_ROWS = COMP_ROWS + PIECE_ROWS
HALF = 64
NEAR = 4
NEAR_SLOTS = ((4, 4), (5, 3), (2, 2), (3, 1))
BASE2_SCALE = DK ** (-0.5) * 1.4426950408889634
NEVER = -jnp.inf
KERNEL_PARAMS = pltpu.CompilerParams(vmem_limit_bytes=32 * 2**20)


def pack_kernel(keys_t, values, pos_k, pos_v, mix_k, mix_v, whole):
    rounds, _, tokens = keys_t.shape
    count = tokens // CMP_BLOCK
    gains_k = jnp.concatenate([pos_k[...].astype(jnp.float32)] * count, axis=0).T
    gains_v = jnp.concatenate([pos_v[...].astype(jnp.float32)] * count, axis=0)
    pooled_k = jnp.zeros((DK, tokens), jnp.float32)
    lane = lax.broadcasted_iota(jnp.int32, (tokens, tokens), 1)
    segment = lax.broadcasted_iota(jnp.int32, (tokens, tokens), 0) // CMP_BLOCK
    pooled_v = []
    for piece in range(rounds):
        base = COMP_ROWS + piece * PIECE_ROWS
        whole[base : base + DK, :] = keys_t[piece]
        whole[base + DK : base + PIECE_ROWS, :] = values[piece]
        product = keys_t[piece].astype(jnp.float32) * gains_k
        upper = product.astype(jnp.bfloat16)
        lower = (product - upper.astype(jnp.float32)).astype(jnp.bfloat16)
        picks = (lane == segment + piece * count).astype(jnp.bfloat16)
        pooled_k += jnp.dot(upper, picks, preferred_element_type=jnp.float32)
        pooled_k += jnp.dot(lower, picks, preferred_element_type=jnp.float32)
        product_v = values[piece].astype(jnp.float32) * gains_v
        pooled_v.append(jnp.sum(product_v.reshape(count, CMP_BLOCK, DV), axis=1))
    comp_k = lax.dot_general(
        pooled_k.astype(jnp.bfloat16),
        mix_k[...],
        (((0,), (0,)), ((), ())),
        preferred_element_type=jnp.float32,
    )[: rounds * count]
    comp_v = jnp.dot(
        jnp.concatenate(pooled_v, axis=0).astype(jnp.bfloat16),
        mix_v[...],
        preferred_element_type=jnp.float32,
    )
    comp_k = jnp.concatenate([comp_k, jnp.zeros((rounds * count, HALF), jnp.float32)], axis=1)
    rows = [comp_k[:, :DV], comp_k[:, DV:], comp_v]
    rows.append(jnp.zeros((COMP_ROWS - 3 * rounds * count, DV), jnp.float32))
    packed = jnp.concatenate(rows, axis=0).astype(jnp.bfloat16)
    whole[:COMP_ROWS, :] = packed


def holder_of(slot, myself, devices):
    source = lax.rem(myself // PAIR - slot // PAIR + devices // PAIR, devices // PAIR) * PAIR
    side = lax.rem(myself, PAIR)
    return source + (side if slot % PAIR == 0 else 1 - side)


def add(scores, mask):
    shape = (scores.shape[0] // mask.shape[0],) + mask.shape
    return (scores.reshape(shape) + mask[None]).reshape(scores.shape)


def prepare_kernel(devices, me_ref, q_ref, gate_ref, sel_ref, q_out, gate_wide, bias, comp_bias, done):
    groups = sel_ref.shape[0]
    tokens = groups * QBLOCK
    per_slot = 2 * tokens // CMP_BLOCK
    myself = me_ref[0]
    copy = pltpu.make_async_copy(q_ref, q_out, done)
    copy.start()
    gates = jax.nn.sigmoid(gate_ref[...].astype(jnp.float32))
    pad = jnp.zeros((2 * HALF - 3 * HEADS, tokens), jnp.float32)
    gates = jnp.concatenate([gates, pad], axis=0).T
    for column in range(3 * HEADS):
        spread = jnp.broadcast_to(gates[:, column : column + 1], (tokens, DV))
        gate_wide[:, column * DV : (column + 1) * DV] = spread
    ids = sel_ref[...]
    entry = lax.broadcasted_iota(jnp.int32, ids.shape, 1)
    lane = lax.broadcasted_iota(jnp.int32, (groups, tokens), 1)
    for slot in range(devices):
        first = holder_of(slot, myself, devices) * (tokens // SEL_BLOCK)
        row = jnp.full((groups, tokens), NEVER, jnp.float32)
        for block in range(tokens // SEL_BLOCK):
            found = jnp.where((ids == first + block) & (entry > 0), 1, 0)
            named = jnp.max(found, axis=1, keepdims=True) > 0
            row = jnp.where((lane // SEL_BLOCK == block) & named, 0.0, row)
        spread = jnp.broadcast_to(row[:, None, :], (groups, QBLOCK, tokens))
        bias[slot] = spread.reshape(tokens, tokens)
    query = lax.broadcasted_iota(jnp.int32, (tokens, tokens), 0)
    key_at = lax.broadcasted_iota(jnp.int32, (tokens, tokens), 1)
    same = key_at // SEL_BLOCK == query // SEL_BLOCK
    bias[devices] = jnp.where((key_at <= query) & same, 0.0, NEVER)
    column = lax.broadcasted_iota(jnp.int32, comp_bias.shape, 1)
    offset = lax.broadcasted_iota(jnp.int32, comp_bias.shape, 0)
    within = lax.rem(column, per_slot) - per_slot // 2
    ready = jnp.full(column.shape, -1, jnp.int32)
    for slot in range(devices):
        holder = holder_of(slot, myself, devices)
        late = jnp.where(holder > myself, tokens, -1)
        end = jnp.where(holder == myself, (within + 1) * CMP_BLOCK - 1, late)
        ready = jnp.where((column // per_slot == slot) & (within >= 0), end, ready)
    comp_bias[...] = jnp.where(ready <= offset, 0.0, NEVER)
    copy.wait()


def attend_call(devices, slots, near, args, carried, messages):
    me, queries, gate_wide, masks, comp_mask = args
    first_pass = carried is None
    tokens = queries.shape[0]
    per_slot = 2 * tokens // CMP_BLOCK
    near_width = (len(near) + first_pass) * tokens
    far_width = (len(slots) + first_pass) * tokens
    numbers = sorted(set(slots) | {0} if first_pass else messages)
    step_heads, unit_heads, lag = (8, 2, 1) if first_pass else (8, 2, 2)
    steps = HEADS // step_heads

    def kernel(*refs):
        refs = list(refs)
        me_ref, q_ref, mask_ref = refs[:3]
        del refs[:3]
        gate_ref, comp_bias = (None, None) if first_pass else (refs.pop(0), refs.pop(0))
        state = None if first_pass else [refs.pop(0) for _ in range(4)]
        pieces = {slot: refs.pop(0) for slot in numbers}
        if not first_pass:
            pieces[devices - 1] = pieces[devices - 2].at[pl.ds(CACHED_ROWS, CACHED_ROWS)]
        outs = [refs.pop(0) for _ in range(4 if first_pass else 1)]
        far_low, far_high, far_values, near_low, near_high, near_values = refs[:6]
        if not first_pass:
            comp_low, comp_high, comp_values = refs[6:]
        tables = ((far_low, far_high, far_values), (near_low, near_high, near_values))
        step = pl.program_id(0) * step_heads
        myself = me_ref[0]
        query = lax.broadcasted_iota(jnp.int32, (tokens, tokens), 0)
        key_at = lax.broadcasted_iota(jnp.int32, (tokens, tokens), 1)

        def stage(table, at, piece, start):
            low, high, value = tables[table]
            lanes = slice(at * tokens, (at + 1) * tokens)
            part = piece[pl.ds(start, PIECE_ROWS), :]
            low[:DK, lanes] = part[:DK]
            high[HALF:, lanes] = part[:DK]
            value[lanes, :DV] = part[DK:]

        @pl.when(pl.program_id(0) == 0)
        def _():
            for low, high, value in tables:
                nothing = jnp.zeros((HALF, low.shape[1]), jnp.bfloat16)
                low[DK:, :] = nothing
                high[:HALF, :] = nothing
                value[:, DV:] = jnp.ones((value.shape[0], DV), jnp.bfloat16)
            for at, slot in enumerate(slots):
                stage(0, at, pieces[slot], COMP_ROWS)
            side = lax.rem(myself, PAIR)
            for at, place in enumerate(near):
                choices = NEAR_SLOTS[place]
                in_span = (myself - (NEAR - place) >= 0).astype(jnp.int32)
                start = pl.multiple_of(COMP_ROWS + in_span * PIECE_ROWS, 16)
                if choices[0] == choices[1]:
                    stage(1, at, pieces[choices[0]], start)
                else:
                    for value, slot in enumerate(choices):
                        pl.when(side == value)(
                            lambda at=at, slot=slot, start=start: stage(1, at, pieces[slot], start)
                        )
            if first_pass:
                stage(0, len(slots), pieces[0], CACHED_ROWS)
                stage(1, len(near), pieces[0], CACHED_ROWS)
                return
            comp_values[:, DV:] = jnp.ones((devices * per_slot, DV), jnp.bfloat16)
            for slot in range(devices):
                rows = slice(slot * per_slot, (slot + 1) * per_slot)
                part = pieces[slot][:COMP_ROWS, :].astype(jnp.float32)
                both = jnp.concatenate([part[:per_slot], part[per_slot : 2 * per_slot]], axis=1)
                comp_low[rows, :] = both
                comp_high[rows, :] = pltpu.roll(both, HALF, 1)
                comp_values[rows, :DV] = part[2 * per_slot : 3 * per_slot].astype(jnp.bfloat16)

        def gathered(ref, heads):
            lanes = [pl.ds(pl.multiple_of((step + h) * DV, DV), DV) for h in heads]
            return jnp.concatenate([ref[:, at] for at in lanes], axis=0)

        def score(odd, heads, kind):
            starts = [pl.multiple_of(step * DK + h * DK - odd * HALF, DV) for h in heads]
            rows = jnp.concatenate([q_ref[:, pl.ds(at, 2 * DV)] for at in starts], axis=0)
            if kind == "far":
                table = far_high if odd else far_low
                scores = jnp.dot(rows, table[...], preferred_element_type=jnp.float32)
                masks_of = list(slots) + [devices] * first_pass
                bias = jnp.concatenate([mask_ref[slot] for slot in masks_of], axis=1)
                return [add(scores, bias)]
            if kind == "comp":
                table = (comp_high if odd else comp_low)[...].astype(jnp.bfloat16)
                scores = lax.dot_general(
                    rows, table, (((1,), (1,)), ((), ())), preferred_element_type=jnp.float32
                )
                return [add(scores, comp_bias[...])]
            table = near_high if odd else near_low
            scores = jnp.dot(rows, table[...], preferred_element_type=jnp.float32)
            parts = [scores[:, at * tokens : (at + 1) * tokens] for at in range(near_width // tokens)]
            if first_pass:
                parts[0] = add(parts[0], jnp.where(key_at > query, 0.0, NEVER))
                parts[-1] = add(parts[-1], jnp.where(key_at <= query, 0.0, NEVER))
            return parts

        def weigh(heads, kind, scores):
            highest = scores[0].max(axis=1, keepdims=True)
            for part in scores[1:]:
                highest = jnp.maximum(highest, part.max(axis=1, keepdims=True))
            highest = jnp.broadcast_to(highest, (highest.shape[0], DV))
            if kind != "comp" and not first_pass:
                highest = jnp.maximum(highest, gathered(state[branch_of[kind] + 1], heads))
            weights = []
            for part in scores:
                copies = max(part.shape[1] // DV, 1)
                wide = jnp.concatenate([highest] * copies, axis=1)[:, : part.shape[1]]
                weights.append(jnp.exp2((part - wide) * BASE2_SCALE).astype(jnp.bfloat16))
            return highest, weights

        def mix(heads, kind, highest, weights):
            taken = jnp.concatenate(weights, axis=1) if len(weights) > 1 else weights[0]
            value = far_values if kind == "far" else near_values if kind == "near" else comp_values
            both = jnp.dot(taken, value[...], preferred_element_type=jnp.float32)
            mixed, total = both[:, :DV], both[:, DV:]
            if first_pass:
                return mixed / total, highest + jnp.log(total) * DK**0.5
            if kind != "comp":
                branch = branch_of[kind]
                fade = jnp.exp2((gathered(state[branch + 1], heads) - highest) * BASE2_SCALE)
                mixed, total = mixed + gathered(state[branch], heads) * fade, total + fade
            return mixed / total

        branch_of = {"far": 0, "near": 2}
        kinds = ("far", "near") if first_pass else ("comp", "far", "near")
        units = []
        for odd in range(2):
            for first in range(odd, step_heads, unit_heads * 2):
                heads = list(range(first, first + 2 * unit_heads, 2))
                units += [(odd, heads, kind) for kind in kinds[::-1]]
        found, scored, weighed = {}, {}, {}
        for turn in range(len(units) + 2 * lag):
            if turn < len(units):
                scored[turn] = score(*units[turn])
            at = turn - lag
            if 0 <= at < len(units):
                weighed[at] = weigh(*units[at][1:], scored.pop(at))
            at = turn - 2 * lag
            if 0 <= at < len(units):
                _, heads, kind = units[at]
                found[kind] = mix(heads, kind, *weighed.pop(at))
                if len(found) < len(kinds):
                    continue
                for which, head in enumerate(heads):
                    lines = slice(which * tokens, (which + 1) * tokens)
                    if first_pass:
                        lanes = pl.ds(pl.multiple_of((step + head) * DV, DV), DV)
                        for out, part in zip(outs, found["far"] + found["near"]):
                            out[:, lanes] = part[lines]
                        continue
                    total = 0.0
                    for b, kind in enumerate(kinds):
                        column = b * HEADS + head + step
                        lanes = pl.ds(pl.multiple_of(column * DV, DV), DV)
                        total += gate_ref[:, lanes] * found[kind][lines]
                    outs[0][:, head * DV : (head + 1) * DV] = total.astype(jnp.bfloat16)
                found = {}

    in_vmem = pl.BlockSpec(memory_space=pltpu.VMEM)
    by_head = pl.BlockSpec((tokens, step_heads * DV), lambda i: (0, i))
    in_specs = [
        pl.BlockSpec(memory_space=pltpu.SMEM),
        in_vmem,
        in_vmem,
    ]
    operands = [me, queries, masks]
    if not first_pass:
        in_specs += [in_vmem] * 2
        operands += [gate_wide, comp_mask]
    if not first_pass:
        in_specs += [in_vmem] * 4
        operands += carried
    for slot in numbers:
        in_specs.append(in_vmem)
        operands.append(pltpu.with_memory_space_constraint(messages[slot], pltpu.VMEM))
    scratch = [
        pltpu.VMEM((2 * DV, far_width), jnp.bfloat16),
        pltpu.VMEM((2 * DV, far_width), jnp.bfloat16),
        pltpu.VMEM((far_width, 2 * DV), jnp.bfloat16),
        pltpu.VMEM((2 * DV, near_width), jnp.bfloat16),
        pltpu.VMEM((2 * DV, near_width), jnp.bfloat16),
        pltpu.VMEM((near_width, 2 * DV), jnp.bfloat16),
    ]
    if not first_pass:
        scratch += [
            pltpu.VMEM((devices * per_slot, 2 * DV), jnp.float32),
            pltpu.VMEM((devices * per_slot, 2 * DV), jnp.float32),
            pltpu.VMEM((devices * per_slot, 2 * DV), jnp.bfloat16),
        ]
    partial = [pltpu.VMEM((tokens, HEADS * DV), jnp.float32)] * 4
    columns = far_width + near_width
    return pl.pallas_call(
        kernel,
        grid=(steps,),
        in_specs=in_specs,
        out_specs=[in_vmem] * 4 if first_pass else by_head,
        out_shape=partial if first_pass else jax.ShapeDtypeStruct((tokens, HEADS * DV), jnp.bfloat16),
        scratch_shapes=scratch,
        cost_estimate=pl.CostEstimate(
            flops=2 * tokens * HEADS * columns * (DK + DV),
            transcendentals=tokens * HEADS * columns,
            bytes_accessed=2 * queries.size,
        ),
        compiler_params=KERNEL_PARAMS,
    )(*operands)


EARLY = (0, 1, 2, 3, 4)


def dense_body(queries, keys, values, gate_logits, sel_ids, pos_k, pos_v, mix_k, mix_v):
    devices = lax.axis_size("ctx")
    tokens = keys.shape[1]
    rows = CACHED_ROWS + PIECE_ROWS
    message = pl.pallas_call(
        pack_kernel,
        out_shape=pltpu.VMEM((rows, tokens), jnp.bfloat16),
        name="pack",
    )(jnp.swapaxes(keys, 1, 2), values, pos_k, pos_v, mix_k, mix_v)

    in_vmem = pl.BlockSpec(memory_space=pltpu.VMEM)
    messages = {0: message}
    far_slot = devices - PAIR
    for slot in range(0, far_slot, PAIR):
        if slot > 0:
            messages[slot] = shifted(message, "ctx", slot)
        pairs = [(i, i ^ 1) for i in range(devices)]
        messages[slot + 1] = lax.ppermute(messages[slot], "ctx", pairs)
    both = jnp.concatenate([message[:CACHED_ROWS], messages[1][:CACHED_ROWS]], axis=0)
    messages[far_slot] = shifted(both, "ctx", far_slot)
    me = lax.axis_index("ctx").astype(jnp.int32).reshape(1)
    prepared = pl.pallas_call(
        functools.partial(prepare_kernel, devices),
        in_specs=[pl.BlockSpec(memory_space=pltpu.SMEM), pl.BlockSpec(memory_space=pltpu.HBM)]
        + [in_vmem] * 2,
        out_specs=[in_vmem] * 4,
        out_shape=[
            pltpu.VMEM(queries.shape, queries.dtype),
            pltpu.VMEM((tokens, 3 * HEADS * DV), jnp.float32),
            pltpu.VMEM((devices + 1, tokens, tokens), jnp.float32),
            pltpu.VMEM((tokens, devices * 2 * tokens // CMP_BLOCK), jnp.float32),
        ],
        scratch_shapes=[pltpu.SemaphoreType.DMA],
        name="prepare", compiler_params=KERNEL_PARAMS,
    )(me, queries, gate_logits.T, sel_ids)
    args = (me, *prepared)
    late = tuple(slot for slot in range(devices) if slot not in EARLY)
    state = attend_call(devices, EARLY, (0, 2, 3), args, None, messages)
    return attend_call(devices, late, (1,), args, state, messages)


def body(queries, keys, *others):
    devices = lax.axis_size("ctx")
    rounds, tokens = keys.shape[:2]
    blocks = (rounds - 1) * tokens // SEL_BLOCK * devices
    dense = rounds == 2 and blocks <= SPREAD and devices % PAIR == 0 and devices >= 8
    chosen = dense_body if dense else exchange_body
    return chosen(queries, keys, *others)


def solution(mesh):
    in_specs = (
        P("ctx", "grp"),
        P(None, "ctx", "grp"),
        P(None, "ctx", "grp"),
        P("ctx", "grp"),
        P("ctx", "grp"),
        P(None, "grp"),
        P(None, "grp"),
        P(None, "grp"),
        P(None, "grp"),
    )
    out_specs = P("ctx", "grp")
    return jax.shard_map(body, mesh=mesh, in_specs=in_specs, out_specs=out_specs, check_vma=False)
```
